32 devices in a mesh: dp: 8 (over y, x, core), tensor: 4 (over z).
Axes of the slice: x: 2, y: 2, z: 4, core: 2. Of those that a mesh axis runs over, the one named last changes fastest.
Arguments:
- inputs: bfloat16 [16384, 1024], P(('dp', 'tensor')), may hold values from -6 to 6
- lengths: int32 [8], P('dp'), may hold values from 1024 to 2048, as said below
- query_weight: bfloat16 [1024, 1024], P('dp', 'tensor'), may hold values from -0.1875 to 0.1875
- key_weight: bfloat16 [1024, 1024], P('dp', 'tensor'), may hold values from -0.1875 to 0.1875
- value_weight: bfloat16 [1024, 1024], P('dp', 'tensor'), may hold values from -0.1875 to 0.1875
- query_bias: bfloat16 [16, 64], P('tensor', 'dp'), may hold values from -3 to 3
- value_bias: bfloat16 [16, 64], P('tensor', 'dp'), may hold values from -0.29882812 to 0.29882812
- output_weight: bfloat16 [1024, 1024], P('tensor', 'dp'), may hold values from -4 to 4
- output_bias: float32 [1024], P(('dp', 'tensor')), may hold values from -3 to 3
- first_gain: float32 [1024], P(('dp', 'tensor')), may hold values from 0.5 to 1.5
- first_shift: float32 [1024], P(('dp', 'tensor')), may hold values from -1 to 1
- inner_weight: bfloat16 [1024, 4096], P('dp', 'tensor'), may hold values from -0.1875 to 0.1875
- inner_bias: bfloat16 [64, 64], P('tensor', 'dp'), may hold values from -3 to 3
- outer_weight: bfloat16 [4096, 1024], P('tensor', 'dp'), may hold values from -0.09375 to 0.09375
- outer_bias: float32 [1024], P(('dp', 'tensor')), may hold values from -3 to 3
- second_gain: float32 [1024], P(('dp', 'tensor')), may hold values from 0.5 to 1.5
- second_shift: float32 [1024], P(('dp', 'tensor')), may hold values from -1 to 1
- cotangent: bfloat16 [16384, 1024], P(('dp', 'tensor')), may hold values from -6 to 6
Outputs:
- layer_output: bfloat16 [16384, 1024], P(('dp', 'tensor'))
- input_grad: float32 [16384, 1024], P(('dp', 'tensor'))
- query_weight_grad: float32 [1024, 1024], P('dp', 'tensor')
- key_weight_grad: float32 [1024, 1024], P('dp', 'tensor')
- value_weight_grad: float32 [1024, 1024], P('dp', 'tensor')
- query_bias_grad: float32 [16, 64], P('tensor', 'dp')
- value_bias_grad: float32 [16, 64], P('tensor', 'dp')
- output_weight_grad: float32 [1024, 1024], P('tensor', 'dp')
- output_bias_grad: float32 [1024], P(('dp', 'tensor'))
- first_gain_grad: float32 [1024], P(('dp', 'tensor'))
- first_shift_grad: float32 [1024], P(('dp', 'tensor'))
- inner_weight_grad: float32 [1024, 4096], P('dp', 'tensor')
- inner_bias_grad: float32 [64, 64], P('tensor', 'dp')
- outer_weight_grad: float32 [4096, 1024], P('tensor', 'dp')
- outer_bias_grad: float32 [1024], P(('dp', 'tensor'))
- second_gain_grad: float32 [1024], P(('dp', 'tensor'))
- second_shift_grad: float32 [1024], P(('dp', 'tensor'))
The draws below stay inside these ranges and needn't reach their ends.
Inputs may be any that keep to these rules, and one draw needn't show every extreme that they name: `lengths`: each sequence's length; one sequence has exactly 2048 and one exactly 1024.
All inputs are finite; a program needn't handle non-finite values.
Results may differ from the reference program's by a relative error of at most 0.018.
Values may be sent and summed in bfloat16 or wider, within the bound.
A program may use at most 128 MiB of HBM per device.

```python
import jax
import jax.numpy as jnp
from jax import lax

D = 1024
HEADS = 16
HEAD_DIM = 64
FF = 4096
SEQ_LEN = 2048
NSEQ = 8
TOKENS = 16384


def draw_lengths(key, part):
    first, second, third = jax.random.split(key, 3)
    drawn = jax.random.randint(first, (NSEQ,), SEQ_LEN // 2, SEQ_LEN + 1, dtype=jnp.int32)
    longest = jax.random.randint(second, (), 0, NSEQ, dtype=jnp.int32)
    offset = jax.random.randint(third, (), 1, NSEQ, dtype=jnp.int32)
    shortest = (longest + offset) % NSEQ
    places = jnp.arange(NSEQ, dtype=jnp.int32)
    drawn = jnp.where(places == longest, SEQ_LEN, drawn)
    return jnp.where(places == shortest, SEQ_LEN // 2, drawn).astype(jnp.int32)


def with_spikes(values, own_key, source, target, blocks, factor):
    def block_of(position):
        return (jnp.arange(values.shape[position]) // (values.shape[position] // blocks)).reshape((-1,) + (1,) * (values.ndim - 1 - position))

    near = jax.random.permutation(own_key, blocks)[block_of(target)]
    other_side = (block_of(target) + blocks // 2) % blocks
    return jnp.where((block_of(source) == near) | (block_of(source) == other_side), factor * values, values)


def block_levels(stream_key, shape, cuts, low, top_value):
    factor_of, own = 1.0, jax.random.fold_in(stream_key, 6)
    for position, parts in cuts:
        draws = jnp.exp(jax.random.uniform(jax.random.fold_in(own, position), (parts,), jnp.float32, low / len(cuts), top_value / len(cuts)))
        factor_of = factor_of * jnp.repeat(draws, shape[position] // parts).reshape([-1 if axis == position else 1 for axis in range(len(shape))])
    return factor_of


def noise(own_key, dims, width, most, pieces=(), kind=jnp.bfloat16):
    values = jax.random.normal(own_key, dims, jnp.float32) * width
    if len(pieces) > 0:
        values = block_levels(own_key, dims, pieces, -0.22, 0.18) * values
    return jnp.clip(values, min=-most, max=most).astype(kind)


def heavy_noise(key, dims, deviation, limit, cuts, heavy, kind=jnp.bfloat16):
    values = deviation * jax.random.normal(key, dims, jnp.float32)
    if cuts:
        values = values * block_levels(key, dims, cuts, -0.22, 0.18)
    return jnp.clip(with_spikes(values, jax.random.fold_in(key, 3), *heavy), -limit, limit).astype(kind)


def setup_inputs(seed: int = 0) -> dict:
    seeds = jax.random.split(jax.random.key(seed), 19)
    return {
        "inputs": heavy_noise(seeds[0], (TOKENS, D), 1.0, 6.0, ((0, 32),), (0, 1, 32, 2.75)),
        "lengths": draw_lengths(jax.random.fold_in(seeds[18], 71), 0),
        "query_weight": noise(seeds[2], (D, D), D ** -0.5, 0.1875, ((0, 8), (1, 4))),
        "key_weight": noise(seeds[3], (D, D), D ** -0.5, 0.1875, ((0, 8), (1, 4))),
        "value_weight": noise(seeds[4], (D, D), D ** -0.5, 0.1875, ((0, 8), (1, 4))),
        "query_bias": noise(seeds[5], (HEADS, HEAD_DIM), 0.5, 3.0, ((0, 4), (1, 8))),
        "value_bias": noise(seeds[6], (HEADS, HEAD_DIM), 0.05, 0.29882812, ((0, 4), (1, 8))),
        "output_weight": noise(seeds[7], (D, D), (4 * D // SEQ_LEN) ** -0.5, 4.0, ((0, 4), (1, 8))),
        "output_bias": noise(seeds[8], (D,), 0.5, 3.0, ((0, 32),), jnp.float32),
        "first_gain": jnp.clip(1.0 + 0.1 * jax.random.normal(seeds[9], (D,), jnp.float32), 0.5, 1.5),
        "first_shift": noise(seeds[10], (D,), 0.2, 1.0, ((0, 32),), jnp.float32),
        "inner_weight": noise(seeds[11], (D, FF), D ** -0.5, 0.1875, ((0, 8), (1, 4))),
        "inner_bias": noise(seeds[12], (FF // HEAD_DIM, HEAD_DIM), 0.5, 3.0, ((0, 4), (1, 8))),
        "outer_weight": noise(seeds[13], (FF, D), FF ** -0.5, 0.09375, ((0, 4), (1, 8))),
        "outer_bias": noise(seeds[14], (D,), 0.5, 3.0, ((0, 32),), jnp.float32),
        "second_gain": jnp.clip(1.0 + 0.1 * jax.random.normal(seeds[15], (D,), jnp.float32), 0.5, 1.5),
        "second_shift": noise(seeds[16], (D,), 0.2, 1.0, ((0, 32),), jnp.float32),
        "cotangent": heavy_noise(seeds[17], (TOKENS, D), 1.0, 6.0, ((0, 32),), (0, 1, 32, 2.75)),
    }


EPSILON = 1e-12
NEG_LARGE = 1000000000.0
HIGHEST = lax.Precision.HIGHEST

@jax.custom_vjp
def low(v):
    return lax.optimization_barrier(v.astype(jnp.bfloat16)).astype(jnp.float32)

@jax.custom_vjp
def low_back(v):
    return v

def low_keep(v):
    return (low(v), None)

def low_pass(kept, grad):
    return (grad,)

def back_keep(v):
    return (v, None)

def back_low(kept, grad):
    return (low(grad),)
low.defvjp(low_keep, low_pass)
low_back.defvjp(back_keep, back_low)

def layer_norm(hidden, gain, shift):
    center = hidden - lax.optimization_barrier(jnp.mean(hidden, -1, keepdims=True))
    variance = lax.optimization_barrier(jnp.mean(center * center, -1, keepdims=True))
    return center * lax.rsqrt(variance + EPSILON) * gain + shift

def attention_block(query_block, key_heads, value_heads, key_bias):
    raw_scores = jnp.einsum('hqd,hkd->hqk', query_block, key_heads, precision=HIGHEST)
    scores = low_back(raw_scores) * HEAD_DIM ** (-0.5) + key_bias
    probs = jax.nn.softmax(scores, axis=-1)
    return jnp.einsum('hqk,hkd->hqd', low(probs), value_heads, precision=HIGHEST)
checkpointed = jax.checkpoint(attention_block)

def to_heads(matrix):
    return matrix.reshape(SEQ_LEN, HEADS, HEAD_DIM).transpose(1, 0, 2)

def forward_group(params, seq_inputs, length):
    query_weight, key_weight, value_weight, query_bias, value_bias, output_weight, output_bias, first_gain, first_shift, inner_weight, inner_bias, outer_weight, outer_bias, second_gain, second_shift = params
    positions = jnp.arange(SEQ_LEN, dtype=jnp.int32)
    valid = (positions < length).astype(jnp.float32)
    key_bias = (valid - 1.0) * NEG_LARGE
    query_rows = low(low_back(jnp.dot(seq_inputs, query_weight, precision=HIGHEST) + query_bias.reshape(-1)))
    key_rows = low(low_back(jnp.dot(seq_inputs, key_weight, precision=HIGHEST)))
    value_rows = low(low_back(jnp.dot(seq_inputs, value_weight, precision=HIGHEST) + value_bias.reshape(-1)))
    block_rows = min(512, SEQ_LEN)
    block_count = SEQ_LEN // block_rows
    query_blocks = to_heads(query_rows).reshape(HEADS, block_count, block_rows, HEAD_DIM).transpose(1, 0, 2, 3)
    key_heads = to_heads(key_rows)
    value_heads = to_heads(value_rows)
    context = lax.map(lambda query_block: checkpointed(query_block, key_heads, value_heads, key_bias), query_blocks)
    context = context.transpose(0, 2, 1, 3).reshape(SEQ_LEN, D)
    context_low = low(low_back(context))
    attention_out = low_back(jnp.dot(context_low, output_weight, precision=HIGHEST))
    hidden_one = seq_inputs + attention_out + output_bias
    middle = layer_norm(hidden_one, first_gain, first_shift)
    middle_low = low(middle)
    pre_act = low_back(jnp.dot(middle_low, inner_weight, precision=HIGHEST) + inner_bias.reshape(-1))
    act_low = low(jax.nn.gelu(pre_act, approximate=False))
    mlp_out = low_back(jnp.dot(act_low, outer_weight, precision=HIGHEST))
    hidden_two = middle + mlp_out + outer_bias
    return layer_norm(hidden_two, second_gain, second_shift) * valid[:, None]

def reference(inputs, lengths, query_weight, key_weight, value_weight, query_bias, value_bias, output_weight, output_bias, first_gain, first_shift, inner_weight, inner_bias, outer_weight, outer_bias, second_gain, second_shift, cotangent):
    params = tuple((array.astype(jnp.float32) for array in (query_weight, key_weight, value_weight, query_bias, value_bias, output_weight, output_bias, first_gain, first_shift, inner_weight, inner_bias, outer_weight, outer_bias, second_gain, second_shift)))
    seq_all = inputs.astype(jnp.float32).reshape(NSEQ, SEQ_LEN, D)
    cot_all = cotangent.astype(jnp.float32).reshape(NSEQ, SEQ_LEN, D)

    def one_sequence(totals, item):
        seq_inputs, seq_cot, length = item

        def forward_fn(param_set, values):
            return forward_group(param_set, values, length)
        result, pull = jax.vjp(forward_fn, params, seq_inputs)
        grad_params, grad_inputs = pull(seq_cot)
        totals = jax.tree.map(lambda left, right: left + right, totals, grad_params)
        return (totals, (result.astype(jnp.bfloat16), grad_inputs))
    totals, (outputs, input_grads) = lax.scan(one_sequence, jax.tree.map(jnp.zeros_like, params), (seq_all, cot_all, lengths))
    return (outputs.reshape(TOKENS, D), input_grads.reshape(TOKENS, D), totals[0], totals[1], totals[2], totals[3], totals[4], totals[5], totals[6], totals[7], totals[8], totals[9], totals[10], totals[11], totals[12], totals[13], totals[14])
```

```python
import jax
import jax.numpy as jnp
from jax import lax
from jax.experimental import pallas as pl
from jax.experimental.pallas import tpu as pltpu
from jax.sharding import PartitionSpec as P

HEAD_DIM = 64


EPSILON = 1e-12
NEG_LARGE = 1000000000.0


def contract_rows(left, right):
    return lax.dot_general(
        left, right, (((0,), (0,)), ((), ())), preferred_element_type=jnp.float32
    )


def contract_cols(left, right):
    return lax.dot_general(
        left, right, (((1,), (1,)), ((), ())), preferred_element_type=jnp.float32
    )


def plain_product(left, right):
    return jnp.dot(left, right, preferred_element_type=jnp.float32)


def gelu_exact(value):
    return jax.nn.gelu(value, approximate=False)


def norm_forward(hidden, gain, shift):
    center = hidden - jnp.mean(hidden, -1, keepdims=True)
    inverse = lax.rsqrt(jnp.mean(center * center, -1, keepdims=True) + EPSILON)
    normed = center * inverse
    return (normed * gain + shift, normed, inverse)


def norm_backward(grad_out, normed, inverse, gain):
    grad_norm = grad_out * gain
    grad_hidden = inverse * (
        grad_norm
        - jnp.mean(grad_norm, -1, keepdims=True)
        - normed * jnp.mean(grad_norm * normed, -1, keepdims=True)
    )
    return (grad_hidden, jnp.sum(grad_out * normed, 0), jnp.sum(grad_out, 0))


LANES = 128
SCALE = HEAD_DIM ** (-0.5)
EVERY = ("tensor", "dp")


def lane_index(shape):
    return lax.broadcasted_iota(jnp.int32, shape, 1)


def in_half(lane, half):
    return (lane >= half * HEAD_DIM) & (lane < (half + 1) * HEAD_DIM)


def split_three(value):
    first = value.astype(jnp.bfloat16).astype(jnp.float32)
    second = (value - first).astype(jnp.bfloat16).astype(jnp.float32)
    third = (value - first - second).astype(jnp.bfloat16).astype(jnp.float32)
    return (first, second, third)


def key_bias_column(length, rows):
    position = lax.broadcasted_iota(jnp.int32, (rows, LANES), 0)
    return jnp.where(position < length, 0.0, -NEG_LARGE)


def forward_kernel(length_ref, q_ref, k_ref, v_ref, context_ref, logsum_ref, key_aug, value_aug):
    rows, seq_len = (q_ref.shape[0], k_ref.shape[0])

    @pl.when(pl.program_id(1) == 0)
    def prepare():
        lane = lane_index((seq_len, LANES))
        bias = key_bias_column(length_ref[0], seq_len)
        keys = k_ref[...].astype(jnp.float32)
        values = v_ref[...].astype(jnp.float32)
        for half in range(2):
            own = in_half(lane, half)
            spare = HEAD_DIM * (1 - half)
            key_aug[half] = jnp.where(
                own, keys, jnp.where(lane == spare, bias, 0.0)
            ).astype(jnp.bfloat16)
            value_aug[half] = jnp.where(
                own, values, jnp.where(lane == spare, 1.0, 0.0)
            ).astype(jnp.bfloat16)

    lane = lane_index((rows, LANES))
    queries = q_ref[...].astype(jnp.float32) * SCALE
    contexts, logsums = ([], [])
    for half in range(2):
        own = in_half(lane, half)
        spare = HEAD_DIM * (1 - half)
        query = jnp.where(own, queries, jnp.where(lane == spare, 1.0, 0.0)).astype(jnp.bfloat16)
        scores = contract_cols(query, key_aug[half])
        highest = jnp.max(scores, -1, keepdims=True)
        weights = jnp.exp(scores - highest).astype(jnp.bfloat16)
        summed = plain_product(weights, value_aug[half])
        totals = summed[:, spare : spare + 1]
        contexts.append(summed / totals)
        logsums.append(highest + jnp.log(totals))
    first = in_half(lane, 0)
    context_ref[...] = jnp.where(first, contexts[0], contexts[1]).astype(jnp.bfloat16)
    logsum_ref[...] = jnp.where(first, logsums[0], logsums[1])


def backward_kernel(
    length_ref,
    q_ref,
    k_ref,
    v_ref,
    context_ref,
    logsum_ref,
    grad_ref,
    dq_ref,
    dk_ref,
    dv_ref,
    key_aug,
    value_aug,
    key_flipped,
    dk_sum,
    dv_sum,
):
    rows, seq_len = (q_ref.shape[0], k_ref.shape[0])
    step = pl.program_id(1)

    @pl.when(step == 0)
    def prepare():
        lane = lane_index((seq_len, LANES))
        bias = key_bias_column(length_ref[0], seq_len)
        keys = k_ref[...].astype(jnp.float32)
        values = v_ref[...].astype(jnp.float32)
        key_flipped[...] = keys.T.astype(jnp.bfloat16)
        for half in range(2):
            own = in_half(lane, half)
            spare = HEAD_DIM * (1 - half)
            after = (lane > spare) & (lane <= spare + 3)
            key_aug[half] = jnp.where(
                own, keys, jnp.where(lane == spare, bias, jnp.where(after, 1.0, 0.0))
            ).astype(jnp.bfloat16)
            value_aug[half] = jnp.where(own, values, jnp.where(after, 1.0, 0.0)).astype(
                jnp.bfloat16
            )
        dk_sum[...] = jnp.zeros_like(dk_sum)
        dv_sum[...] = jnp.zeros_like(dv_sum)

    lane = lane_index((rows, LANES))
    queries = q_ref[...].astype(jnp.float32) * SCALE
    grads = grad_ref[...].astype(jnp.float32)
    product = grads * context_ref[...].astype(jnp.float32)
    logsum_all = logsum_ref[...]
    flipped = []
    for half in range(2):
        own = in_half(lane, half)
        spare = HEAD_DIM * (1 - half)
        delta = jnp.sum(jnp.where(own, product, 0.0), -1, keepdims=True)
        logsum = logsum_all[:, half * HEAD_DIM : half * HEAD_DIM + 1]
        query = jnp.where(own, queries, jnp.where(lane == spare, 1.0, 0.0))
        grad = jnp.where(own, grads, 0.0)
        for place, (less, minus) in enumerate(zip(split_three(-logsum), split_three(-delta))):
            here = lane == spare + 1 + place
            query = jnp.where(here, less, query)
            grad = jnp.where(here, minus, grad)
        query = query.astype(jnp.bfloat16)
        grad = grad.astype(jnp.bfloat16)
        weights = jnp.exp(contract_cols(key_aug[half], query))
        dv_sum[half] += plain_product(weights.astype(jnp.bfloat16), grad)
        grad_scores = (weights * contract_cols(value_aug[half], grad)).astype(jnp.bfloat16)
        dk_sum[half] += plain_product(grad_scores, query)
        flipped.append(
            plain_product(
                key_flipped[half * HEAD_DIM : (half + 1) * HEAD_DIM, :], grad_scores
            )
        )
    dq_ref[...] = (jnp.concatenate(flipped, 0).T * SCALE).astype(jnp.bfloat16)

    @pl.when(step == pl.num_programs(1) - 1)
    def finish():
        first = in_half(lane_index((seq_len, LANES)), 0)
        dk_ref[...] = jnp.where(first, dk_sum[0], dk_sum[1]).astype(jnp.bfloat16)
        dv_ref[...] = jnp.where(first, dv_sum[0], dv_sum[1]).astype(jnp.bfloat16)


def attend_forward(qkv_rows, lengths):
    seq_len, columns = qkv_rows.shape
    width = columns // 3
    pairs = width // LANES
    rows = min(512, seq_len)
    block = pl.BlockSpec((rows, LANES), lambda pair, step: (step, pair))
    return pl.pallas_call(
        forward_kernel,
        grid=(pairs, seq_len // rows),
        in_specs=[
            pl.BlockSpec(memory_space=pltpu.SMEM),
            block,
            pl.BlockSpec((seq_len, LANES), lambda pair, step: (0, pairs + pair)),
            pl.BlockSpec((seq_len, LANES), lambda pair, step: (0, 2 * pairs + pair)),
        ],
        out_specs=[block, block],
        out_shape=[
            jax.ShapeDtypeStruct((seq_len, width), jnp.bfloat16),
            jax.ShapeDtypeStruct((seq_len, width), jnp.float32),
        ],
        scratch_shapes=[pltpu.VMEM((2, seq_len, LANES), jnp.bfloat16)] * 2,
        compiler_params=pltpu.CompilerParams(vmem_limit_bytes=48 * 2**20),
        cost_estimate=pl.CostEstimate(
            flops=16 * seq_len * seq_len * width,
            bytes_accessed=10 * seq_len * width,
            transcendentals=seq_len * seq_len * width // HEAD_DIM,
        ),
        name="attend_forward",
    )(lengths, qkv_rows, qkv_rows, qkv_rows)


def attend_backward(qkv_rows, lengths, context, logsum, grad_context):
    seq_len, columns = qkv_rows.shape
    width = columns // 3
    pairs = width // LANES
    rows = min(256, seq_len)
    block = pl.BlockSpec((rows, LANES), lambda pair, step: (step, pair))
    whole = pl.BlockSpec((seq_len, LANES), lambda pair, step: (0, pair))
    return pl.pallas_call(
        backward_kernel,
        grid=(pairs, seq_len // rows),
        in_specs=[
            pl.BlockSpec(memory_space=pltpu.SMEM),
            block,
            pl.BlockSpec((seq_len, LANES), lambda pair, step: (0, pairs + pair)),
            pl.BlockSpec((seq_len, LANES), lambda pair, step: (0, 2 * pairs + pair)),
            block,
            block,
            block,
        ],
        out_specs=[block, whole, whole],
        out_shape=[jax.ShapeDtypeStruct((seq_len, width), jnp.bfloat16)] * 3,
        scratch_shapes=[
            pltpu.VMEM((2, seq_len, LANES), jnp.bfloat16),
            pltpu.VMEM((2, seq_len, LANES), jnp.bfloat16),
            pltpu.VMEM((LANES, seq_len), jnp.bfloat16),
            pltpu.VMEM((2, seq_len, LANES), jnp.float32),
            pltpu.VMEM((2, seq_len, LANES), jnp.float32),
        ],
        compiler_params=pltpu.CompilerParams(vmem_limit_bytes=48 * 2**20),
        cost_estimate=pl.CostEstimate(
            flops=40 * seq_len * seq_len * width,
            bytes_accessed=20 * seq_len * width,
            transcendentals=seq_len * seq_len * width // HEAD_DIM,
        ),
        name="attend_backward",
    )(lengths, qkv_rows, qkv_rows, qkv_rows, context, logsum, grad_context)


def gather_everywhere(block):
    whole = lax.all_gather(block, EVERY, axis=0, tiled=True)
    return whole.reshape(lax.axis_size("tensor"), -1, block.shape[1])


def scatter_everywhere(blocks):
    rows = lax.axis_size("dp")
    columns = blocks[0].shape[1]
    stacked = jnp.stack([block.reshape(rows, -1, columns) for block in blocks], 1)
    summed = lax.psum_scatter(
        stacked.reshape(-1, columns), "dp", scatter_dimension=0, tiled=True
    )
    return lax.psum_scatter(summed, "tensor", scatter_dimension=0, tiled=True).astype(
        jnp.float32
    )


def exchange(blocks):
    return lax.all_to_all(blocks, "tensor", split_axis=0, concat_axis=0, tiled=True)


def pack_owned(whole, own_shape):
    parts = whole.reshape(whole.shape[0], own_shape[0], -1, own_shape[1])
    return parts.transpose(2, 0, 1, 3).reshape(parts.shape[2], whole.shape[0], -1)


def unpack_owned(pieces, own_shape):
    parts = pieces.reshape(pieces.shape[0], pieces.shape[1], own_shape[0], own_shape[1])
    return parts.transpose(1, 2, 0, 3).reshape(pieces.shape[1], -1)


def body(
    inputs,
    lengths,
    query_weight,
    key_weight,
    value_weight,
    query_bias,
    value_bias,
    output_weight,
    output_bias,
    first_gain,
    first_shift,
    inner_weight,
    inner_bias,
    outer_weight,
    outer_bias,
    second_gain,
    second_shift,
    cotangent,
):
    low = jnp.bfloat16
    local_rows, model = inputs.shape
    tensor_size = lax.axis_size("tensor")
    dp_size = lax.axis_size("dp")
    place = lax.axis_index("tensor")
    positions = jnp.arange(local_rows, dtype=jnp.int32) + place * local_rows
    valid_mine = (positions < lengths[0]).astype(jnp.float32)[:, None]

    small = [query_bias, value_bias, inner_bias]
    vectors = [output_bias, first_gain, first_shift, outer_bias, second_gain, second_shift]
    packed = jnp.concatenate([part.reshape(-1).astype(jnp.float32) for part in small + vectors])
    packed = lax.all_gather(packed[None], ("dp", "tensor"), axis=0, tiled=True)
    packed = packed.reshape(dp_size, tensor_size, -1)
    cut_one = query_bias.size
    cut_two = cut_one + value_bias.size
    cut_three = cut_two + inner_bias.size
    bias_query = unpack_owned(packed[:, :, :cut_one], query_bias.shape)
    bias_value = unpack_owned(packed[:, :, cut_one:cut_two], value_bias.shape)
    bias_inner = unpack_owned(packed[:, :, cut_two:cut_three], inner_bias.shape)
    vectors = packed[:, :, cut_three:].reshape(dp_size * tensor_size, 6, -1)
    vectors = vectors.transpose(1, 0, 2).reshape(6, -1)
    bias_out, gain_one, shift_one, bias_two, gain_two, shift_two = vectors

    width = query_weight.shape[1]
    projections = jnp.concatenate([query_weight, key_weight, value_weight], 1)
    full_projection = lax.all_gather(projections, "dp", axis=0, tiled=True)
    seq_inputs = lax.all_gather(inputs, "tensor", axis=0, tiled=True)
    full_output = gather_everywhere(output_weight.T)
    full_inner = gather_everywhere(inner_weight)
    full_outer = gather_everywhere(outer_weight.T)
    bias_qkv = jnp.concatenate(
        [bias_query[place], jnp.zeros((width,), jnp.float32), bias_value[place]]
    )
    qkv_rows = (plain_product(seq_inputs, full_projection) + bias_qkv).astype(low)
    context, logsum = attend_forward(qkv_rows, lengths)
    context_mine = exchange(context.reshape(tensor_size, local_rows, width))
    attention_mine = sum(
        contract_cols(context_mine[t], full_output[t]) for t in range(tensor_size)
    )
    hidden_one = inputs.astype(jnp.float32) + attention_mine + bias_out
    middle, normed_one, inverse_one = norm_forward(hidden_one, gain_one, shift_one)
    middle_low = middle.astype(low)
    pre_act = [
        plain_product(middle_low, full_inner[t]) + bias_inner[t] for t in range(tensor_size)
    ]
    act_low = [gelu_exact(part).astype(low) for part in pre_act]
    mlp_mine = sum(contract_cols(act_low[t], full_outer[t]) for t in range(tensor_size))
    hidden_two = middle + mlp_mine + bias_two
    final, normed_two, inverse_two = norm_forward(hidden_two, gain_two, shift_two)
    layer_output = (final * valid_mine).astype(low)

    grad_final = cotangent.astype(jnp.float32) * valid_mine
    grad_two, grad_gain_two, grad_shift_two = norm_backward(
        grad_final, normed_two, inverse_two, gain_two
    )
    grad_bias_two = jnp.sum(grad_two, 0)
    grad_two_low = grad_two.astype(low)
    owned_outer = scatter_everywhere(
        [contract_rows(grad_two_low, part).astype(low) for part in act_low]
    ).T
    grad_pre = []
    for t in range(tensor_size):
        grad_act = plain_product(grad_two_low, full_outer[t])
        grad_pre.append(jax.vjp(gelu_exact, pre_act[t])[1](grad_act)[0].astype(low))
    grad_inner_bias = jnp.stack([jnp.sum(part.astype(jnp.float32), 0) for part in grad_pre])
    owned_inner = scatter_everywhere(
        [contract_rows(middle_low, part).astype(low) for part in grad_pre]
    )
    grad_middle = grad_two + sum(
        contract_cols(grad_pre[t], full_inner[t]) for t in range(tensor_size)
    )
    grad_one, grad_gain_one, grad_shift_one = norm_backward(
        grad_middle, normed_one, inverse_one, gain_one
    )
    grad_bias_out = jnp.sum(grad_one, 0)
    grad_one_low = grad_one.astype(low)
    grad_context_mine = jnp.stack(
        [plain_product(grad_one_low, full_output[t]).astype(low) for t in range(tensor_size)]
    )
    owned_output = scatter_everywhere(
        [contract_rows(grad_one_low, context_mine[t]).astype(low) for t in range(tensor_size)]
    ).T
    grad_context = exchange(grad_context_mine).reshape(-1, width)
    grad_vectors = jnp.stack(
        [
            grad_bias_out,
            grad_gain_one,
            grad_shift_one,
            grad_bias_two,
            grad_gain_two,
            grad_shift_two,
        ]
    )
    grad_vectors = grad_vectors.reshape(6, dp_size * tensor_size, -1).transpose(1, 0, 2)
    grad_vectors = grad_vectors.reshape(dp_size * tensor_size, -1)
    grad_small = pack_owned(
        grad_inner_bias.reshape(tensor_size, inner_bias.shape[0], -1), inner_bias.shape
    ).reshape(dp_size * tensor_size, -1)
    owned_early = lax.psum_scatter(
        jnp.concatenate([grad_small, grad_vectors], 1),
        ("dp", "tensor"),
        scatter_dimension=0,
        tiled=True,
    )[0]
    owned_inner_bias = owned_early[: inner_bias.size].reshape(inner_bias.shape)
    owned_vectors = owned_early[inner_bias.size :].reshape(6, -1)

    grad_qkv = jnp.concatenate(
        attend_backward(qkv_rows, lengths, context, logsum, grad_context), 1
    )
    input_part = contract_cols(grad_qkv, full_projection)
    input_grad = grad_one + lax.psum_scatter(
        input_part.astype(low), "tensor", scatter_dimension=0, tiled=True
    ).astype(jnp.float32)
    owned_projection = lax.psum_scatter(
        contract_rows(seq_inputs, grad_qkv).astype(low), "dp", scatter_dimension=0, tiled=True
    ).astype(jnp.float32)
    sums = jnp.sum(grad_qkv.astype(jnp.float32), 0).reshape(1, 3, -1)
    pieces = [
        pack_owned(sums[:, which].reshape(1, query_bias.shape[0], -1), query_bias.shape)
        for which in (0, 2)
    ]
    owned_biases = lax.psum_scatter(
        jnp.concatenate(pieces, 2).reshape(dp_size, -1), "dp", scatter_dimension=0, tiled=True
    )[0]
    return (
        layer_output,
        input_grad,
        owned_projection[:, :width],
        owned_projection[:, width : 2 * width],
        owned_projection[:, 2 * width :],
        owned_biases[:cut_one].reshape(query_bias.shape),
        owned_biases[cut_one:].reshape(value_bias.shape),
        owned_output,
        owned_vectors[0],
        owned_vectors[1],
        owned_vectors[2],
        owned_inner,
        owned_inner_bias,
        owned_outer,
        owned_vectors[3],
        owned_vectors[4],
        owned_vectors[5],
    )


def solution(mesh):
    placed = (
        P(("dp", "tensor"), None),
        P("dp"),
        P("dp", "tensor"),
        P("dp", "tensor"),
        P("dp", "tensor"),
        P("tensor", "dp"),
        P("tensor", "dp"),
        P("tensor", "dp"),
        P(("dp", "tensor")),
        P(("dp", "tensor")),
        P(("dp", "tensor")),
        P("dp", "tensor"),
        P("tensor", "dp"),
        P("tensor", "dp"),
        P(("dp", "tensor")),
        P(("dp", "tensor")),
        P(("dp", "tensor")),
        P(("dp", "tensor"), None),
    )
    return jax.shard_map(
        body,
        mesh=mesh,
        in_specs=placed,
        out_specs=(
            P(("dp", "tensor"), None),
            P(("dp", "tensor"), None),
            P("dp", "tensor"),
            P("dp", "tensor"),
            P("dp", "tensor"),
            P("tensor", "dp"),
            P("tensor", "dp"),
            P("tensor", "dp"),
            P(("dp", "tensor")),
            P(("dp", "tensor")),
            P(("dp", "tensor")),
            P("dp", "tensor"),
            P("tensor", "dp"),
            P("tensor", "dp"),
            P(("dp", "tensor")),
            P(("dp", "tensor")),
            P(("dp", "tensor")),
        ),
        check_vma=False,
    )
```
